128 devices in a mesh: grp: 4 (over y), atom: 32 (over x, z, core).
Axes of the slice: x: 4, y: 4, z: 4, core: 2. Of those that a mesh axis runs over, the one named last changes fastest.
Arguments:
- tokens: bfloat16 [512, 8192], P(('grp', 'atom')), may hold values from -6 to 6
- dictionary: bfloat16 [32, 2048, 8192], P('atom', None, 'grp'), may hold values from -0.03125 to 0.03125
- candidates: int32 [512, 8], P(('grp', 'atom')), may hold values from 0 to 31, all different within a row; in each aligned block of 4 rows (0 to 3, 4 to 7, ...) at most 2 rows name the same one
Outputs:
- residual: float32 [512, 8192], P(('grp', 'atom'))
- codes: float32 [32, 256, 2048], P('atom', None, 'grp')
The draws below stay inside these ranges and needn't reach their ends.
Inputs may be any that keep to these rules, and one draw needn't show every extreme that they name: `candidates`: each token names 8 different blocks. Among the 4 tokens of one shard (tokens s * 4 to (s + 1) * 4 - 1) no block is named by more than 2 tokens, and some block is named by exactly 2. Every block is named by some token.
All inputs are finite; a program needn't handle non-finite values.
Results may differ from the reference program's by a relative error of at most 0.02.
Values may be sent and summed in bfloat16 or wider, within the bound.
A program may use at most 64 MiB of HBM per device.

```python
import math
import jax
import jax.numpy as jnp
import numpy as np
from jax import lax

D = 8192
ATOMS = 2048
K = 8
ITERS = 2
TOK_DEV = 4
BLOCKS = 32
CAP = 2
TOKENS = 512
SLOTS = 256
FEAT_DEV = 2048
N_GRP = 4


def draw_dictionary(key, part):
    full_shape = (BLOCKS, ATOMS, D)
    spread = (2.0 * D) ** (-0.5)
    values = jnp.clip(jax.random.normal(key, full_shape, jnp.float32), -4.0, 4.0)
    return (values * spread).astype(jnp.bfloat16)


def block_levels(rng, dims, shards, low, top_value):
    factor_of = 1.0
    for axis_at, blocks in shards:
        heights = jax.random.uniform(jax.random.fold_in(jax.random.fold_in(rng, 6), axis_at), (blocks,), jnp.float32, low / len(shards), top_value / len(shards))
        factor_of = factor_of * jnp.repeat(jnp.exp(heights), dims[axis_at] // blocks).reshape((-1,) + (1,) * (len(dims) - 1 - axis_at))
    return factor_of


def shared_out(key, own, number, rows, amount, top, reach, slope):
    sequence = jax.random.permutation(key, amount)
    heavy_load, usual = load_shares(amount, rows * top, reach, slope, True), load_shares(amount, rows * top, reach, slope, False)
    places = jnp.arange(amount)

    def named(sizes, rotation):
        used = int((sizes > 0).sum())
        fixed = max(1, used // 4)
        moved = fixed + (places - fixed + rotation * (used - fixed)) % max(1, amount - fixed)
        return jnp.zeros((amount,), jnp.int32).at[sequence[jnp.where(places < fixed, places, moved)]].set(jnp.asarray(sizes, jnp.int32))

    sizes = jnp.where(number % 4 == 0, named(heavy_load, number // 4), named(usual, number - number // 4 - 1))
    mixed = jax.random.permutation(jax.random.fold_in(own, 3), amount)
    source_of, taker = mixed[0:amount // 2 * 2:2], mixed[1:amount // 2 * 2:2]
    margin = jnp.minimum(sizes[source_of] - 1, reach - sizes[taker]) // 2
    margin = jnp.where((source_of == sequence[0]) | (taker == sequence[0]) | (sizes[taker] == 0), 0, jnp.maximum(margin, 0))
    moved = jax.random.randint(jax.random.fold_in(own, 4), (amount // 2,), 0, 1 << 20) % (margin + 1)
    sizes = sizes.at[source_of].add(-moved).at[taker].add(moved)
    items = jnp.searchsorted(jnp.cumsum(sizes), jnp.arange(rows * top), side="right").astype(jnp.int32)
    grid = items.reshape(top, rows).T
    grid = grid[jax.random.permutation(jax.random.fold_in(own, 1), rows)]
    rotation = jax.random.randint(jax.random.fold_in(own, 2), (rows, 1), 0, top)
    return jnp.take_along_axis(grid, (jnp.arange(top)[None, :] + rotation) % top, axis=1)


def load_shares(amount, total, reach, slope, full):
    weights = [(1 << 20) // math.isqrt(rank ** slope) + 1 for rank in range(1, amount + 1)]
    largest = reach if full else min(reach, max(-(-total // amount), total * weights[0] // sum(weights)))
    least = 1 if total - largest >= amount - 1 else 0
    given, surplus = [largest] + [least] * (amount - 1), total - largest - least * (amount - 1)
    while surplus > 0:
        free = [i for i in range(1, amount) if given[i] < largest] or [i for i in range(1, amount) if given[i] < reach]
        mass, remaining = sum([weights[i] for i in free]), surplus
        for i in free:
            more = min(reach - given[i], max(1, remaining * weights[i] // mass), surplus)
            given[i] = given[i] + more
            surplus = surplus - more
    return np.array(given)


def normal_values(own_key, shape, scale, reach, pieces=(), held_as=jnp.bfloat16):
    values = jax.random.normal(own_key, shape, jnp.float32) * scale
    if len(pieces) > 0:
        values = block_levels(own_key, shape, pieces, -0.22, 0.18) * values
    return jnp.clip(values, min=-reach, max=reach).astype(held_as)


def setup_inputs(seed: int = 0) -> dict:
    arg_keys = jax.random.split(jax.random.key(seed), 4)
    tokens = normal_values(arg_keys[0], (TOKENS, D), 1.0, 6.0, ((0, 128),))
    dictionary = draw_dictionary(jax.random.fold_in(arg_keys[3], 71), 0)
    candidates_keys = jax.random.split(jax.random.fold_in(arg_keys[2], 1), TOKENS // TOK_DEV)
    candidates_turns = jax.random.permutation(jax.random.fold_in(arg_keys[2], 3), TOKENS // TOK_DEV)
    candidates = jax.vmap(lambda own, number: shared_out(jax.random.fold_in(arg_keys[2], 2), own, number, TOK_DEV, BLOCKS, K, CAP, 2))(candidates_keys, candidates_turns).reshape((TOKENS, K))
    return dict(tokens=tokens, dictionary=dictionary, candidates=candidates)


step_size = 1.6
sparsity = 0.125


def rounded(values):
    return lax.optimization_barrier(values.astype(jnp.bfloat16)).astype(jnp.float32)


def slot_numbers(candidates):
    by_shard = candidates.reshape(TOKENS // TOK_DEV, TOK_DEV, K)
    block_ids = jnp.arange(BLOCKS, dtype=jnp.int32)
    member = jnp.sum((by_shard[..., None] == block_ids).astype(jnp.int32), axis=2)
    before = jnp.cumsum(member, axis=1) - member
    picked = jnp.take_along_axis(before, by_shard, axis=2)
    return picked.reshape(TOKENS, K).astype(jnp.int32)


def reference(tokens, dictionary, candidates):
    slot_ids = slot_numbers(candidates)
    shard_ids = (jnp.arange(TOKENS, dtype=jnp.int32) // TOK_DEV)[:, None]
    position = (shard_ids * CAP + slot_ids).astype(jnp.int32)
    initial = tokens.astype(jnp.float32)
    residual = initial
    code_state = jnp.zeros((BLOCKS, SLOTS, ATOMS), jnp.float32)

    def one_block(operands):
        block_rows, code_block, weights = operands
        gradient = jnp.zeros((SLOTS, ATOMS), jnp.float32)
        for feature_part in range(N_GRP):
            lower = feature_part * FEAT_DEV
            upper = lower + FEAT_DEV
            partial_value = jnp.dot(block_rows[:, lower:upper], weights[:, lower:upper].T, preferred_element_type=jnp.float32)
            gradient = gradient + rounded(partial_value)
        code_block = jnp.maximum(code_block + step_size * (gradient - sparsity), 0.0)
        rebuilt = jnp.dot(code_block.astype(jnp.bfloat16), weights, preferred_element_type=jnp.float32).astype(jnp.bfloat16)
        return code_block, rebuilt

    for iteration in range(ITERS):
        outbound = residual.astype(jnp.bfloat16)
        dispatch = jnp.zeros((BLOCKS, SLOTS, D), jnp.bfloat16)
        dispatch = dispatch.at[candidates, position].set(jnp.broadcast_to(outbound[:, None, :], (TOKENS, K, D)))
        code_state, rebuilt_all = lax.map(one_block, (dispatch, code_state, dictionary))
        gathered = rebuilt_all[candidates, position].astype(jnp.float32)
        residual = initial - jnp.sum(gathered, axis=1)
    return residual, code_state
```

```python
import jax
import jax.numpy as jnp
from jax import lax
from jax.experimental import pallas as pl
from jax.experimental.pallas import tpu as pltpu
from jax.sharding import PartitionSpec as P

ITERS = 2
CHAINS = 1
STEP = 1.6
SPARSITY = 0.125
MESH = pl.DeviceIdType.MESH
SHIFT = (0, 3, 1, 2)
BF = jnp.bfloat16
F32 = jnp.float32
N_SEMS = 260
LANES = 128


def nt_dot(a, b):
    return lax.dot_general(a, b, (((1,), (1,)), ((), ())), preferred_element_type=F32)


def nn_dot(a, b):
    return jnp.dot(a, b, preferred_element_type=F32)


def source(me, position):
    shift = jnp.where(position == 1, 3, jnp.where(position == 2, 1, jnp.where(position == 3, 2, 0)))
    return (me + shift) % 4


class Net:
    def __init__(self, send, recv):
        self.send, self.recv, self.count, self.open = send, recv, 0, []

    def copy(self, src, dst, device):
        n = self.count
        self.count += 1
        made = pltpu.make_async_remote_copy(
            src_ref=src,
            dst_ref=dst,
            send_sem=self.send.at[n],
            recv_sem=self.recv.at[n],
            device_id=device,
            device_id_type=MESH,
        )
        made.start()
        self.open.append(made)
        return made

    def finish(self):
        for made in self.open:
            made.wait_send()


def body(names, *refs):
    r = dict(zip(names, refs))
    tok, dict_hbm, res_out, codes = r["tok"], r["dict"], r["res"], r["codes"]
    weights = r["weights"]
    y, atom = lax.axis_index("grp"), lax.axis_index("atom")
    x, z, core = atom // 8, (atom // 2) % 4, atom % 2
    tokens_in = 16 // CHAINS
    shards_in = 4 // CHAINS
    rows = 256 // CHAINS
    gathered = 32 * tokens_in
    half = gathered // 2

    load = pltpu.make_async_copy(dict_hbm.at[0], weights, r["wsem"])
    load.start()

    def device(nx, nz, nc):
        return {"atom": nx * 8 + nz * 2 + nc}

    minus = {"x": device((x + 3) % 4, z, core), "z": device(x, (z + 3) % 4, core), "y": {"grp": (y + 3) % 4}}
    plus = {"x": device((x + 1) % 4, z, core), "z": device(x, (z + 1) % 4, core), "y": {"grp": (y + 1) % 4}}
    partner = device(x, z, 1 - core)
    opposite = {"grp": (y + 2) % 4}

    barrier = pltpu.get_barrier_semaphore()
    others = [minus["x"], plus["x"], minus["z"], plus["z"], minus["y"], plus["y"], opposite, partner]
    for other in others:
        pl.semaphore_signal(barrier, inc=1, device_id=other, device_id_type=MESH)
    pl.semaphore_wait(barrier, len(others))

    net = Net(r["send"], r["recv"])

    first = r["first"]
    swaps = []
    for position in (1, 2, 3):
        target = (y + SHIFT[position]) % 4
        swaps.append(net.copy(tok.at[target], first.at[y], {"grp": target}))
    first[y] = tok[y]

    lo, hi = pl.ds(0, 256), pl.ds(256, 256)

    def gather(big):
        st = []
        for h in range(2):
            g = big[h]
            width = g.shape[-1]
            cut = (width // 2 + LANES - 1) // LANES * LANES
            left, right = pl.ds(0, cut), pl.ds(cut, width - cut)
            full = pl.ds(0, width)
            a, b = ("x", "z") if h == 0 else ("z", "x")

            def view(pa, pb, cols=full, owner=0, g=g, h=h):
                return g.at[owner, pa, pb, :, cols] if h == 0 else g.at[owner, pb, pa, :, cols]

            def share(pa, pb, view=view):
                return net.copy(view(pa, pb), view(pa, pb, owner=1), partner)

            st.append(dict(view=view, share=share, left=left, right=right, a=a, b=b, part=[]))
        mid, every = pl.ds(1, 2), pl.ds(0, 4)
        for s in st:
            v, a, b = s["view"], s["a"], s["b"]
            s["a1"] = net.copy(v(0, 0), v(1, 0), plus[a])
            s["a2"] = net.copy(v(0, 0), v(2, 0), minus[a])
            s["b1"] = net.copy(v(0, 0), v(0, 1), plus[b])
            s["b2"] = net.copy(v(0, 0), v(0, 2), minus[b])
            s["part"].append(s["share"](0, 0))
        yield
        for s in st:
            v, a, b, lf, rt = s["view"], s["a"], s["b"], s["left"], s["right"]
            s["a1"].wait_recv()
            s["fa1"] = net.copy(v(1, 0, lf), v(3, 0, lf), plus[a])
            s["a2"].wait_recv()
            s["fa2"] = net.copy(v(2, 0, rt), v(3, 0, rt), minus[a])
            s["n1"] = net.copy(v(mid, 0), v(mid, 1), plus[b])
            s["n2"] = net.copy(v(mid, 0), v(mid, 2), minus[b])
            s["part"].append(s["share"](mid, 0))
        for s in st:
            v, a, b, lf, rt = s["view"], s["a"], s["b"], s["left"], s["right"]
            s["b1"].wait_recv()
            s["fo1"] = net.copy(v(0, 1, lf), v(0, 3, lf), plus[b])
            s["b2"].wait_recv()
            s["fo2"] = net.copy(v(0, 2, rt), v(0, 3, rt), minus[b])
            s["part"].append(s["share"](0, mid))
        yield
        for s in st:
            v, a, b = s["view"], s["a"], s["b"]
            s["fa1"].wait_recv()
            s["fa2"].wait_recv()
            s["o1"] = net.copy(v(3, 0), v(3, 1), plus[b])
            s["o2"] = net.copy(v(3, 0), v(3, 2), minus[b])
            s["part"].append(s["share"](3, 0))
        yield
        for s in st:
            v, a, b, lf, rt = s["view"], s["a"], s["b"], s["left"], s["right"]
            s["n1"].wait_recv()
            s["fn1"] = net.copy(v(mid, 1, lf), v(mid, 3, lf), plus[b])
            s["n2"].wait_recv()
            s["fn2"] = net.copy(v(mid, 2, rt), v(mid, 3, rt), minus[b])
            s["part"].append(s["share"](mid, mid))
        yield
        for s in st:
            v, a, b, lf, rt = s["view"], s["a"], s["b"], s["left"], s["right"]
            s["o1"].wait_recv()
            s["fp1"] = net.copy(v(3, 1, lf), v(3, 3, lf), plus[b])
            s["o2"].wait_recv()
            s["fp2"] = net.copy(v(3, 2, rt), v(3, 3, rt), minus[b])
            s["part"].append(s["share"](3, mid))
        yield
        for s in st:
            for key in ("fo1", "fo2", "fn1", "fn2", "fp1", "fp2"):
                s[key].wait_recv()
            s["part"].append(s["share"](every, 3))
        yield
        for s in st:
            for made in s["part"]:
                made.wait_recv()

    def ring_sum(axis, view, opp, nbr, cols):
        cut = cols // 2
        left, right = pl.ds(0, cut), pl.ds(cut, cut)
        c_om = net.copy(view(3, left), opp.at[0], plus[axis])
        c_op = net.copy(view(3, right), opp.at[1], minus[axis])
        c_ph = net.copy(view(2, right), view_of(nbr, 0, right), plus[axis])
        c_ml = net.copy(view(1, left), view_of(nbr, 1, left), minus[axis])
        yield
        c_om.wait_recv()
        mine = view(2, left)
        mine[...] = (mine[...].astype(F32) + opp[0].astype(F32)).astype(BF)
        c_pl = net.copy(mine, view_of(nbr, 0, left), plus[axis])
        c_op.wait_recv()
        mine = view(1, right)
        mine[...] = (mine[...].astype(F32) + opp[1].astype(F32)).astype(BF)
        c_mh = net.copy(mine, view_of(nbr, 1, right), minus[axis])
        yield
        for made in (c_ph, c_ml, c_pl, c_mh):
            made.wait_recv()

    def view_of(nbr, side, cols):
        lead = (slice(None),) * (len(nbr.shape) - 2)
        return nbr.at[(side,) + lead + (cols,)]

    def make_selectors(k, sel, sel_t, big):
        tags = big[0][:, :, :, :, 1024:1152].reshape(gathered, LANES)

        def shard_of(g):
            px, pz = (g // (4 * tokens_in)) % 4, (g // tokens_in) % 4
            own = g // (16 * tokens_in)
            column = source(x, px) * 8 + source(z, pz) * 2 + (core + own) % 2
            return ((g // 4) % shards_in + k * shards_in) * 32 + column

        pick = (lax.broadcasted_iota(jnp.int32, (rows, LANES), 1) == atom).astype(BF)
        slot = nt_dot(pick, tags)
        p = lax.broadcasted_iota(jnp.int32, (rows, gathered), 0)
        g = lax.broadcasted_iota(jnp.int32, (rows, gathered), 1)
        hit = (shard_of(g) == p // 2 + k * (rows // 2)) & (slot == (p % 2).astype(F32))
        sel[...] = jnp.where(hit, 1.0, 0.0).astype(BF)
        q = lax.broadcasted_iota(jnp.int32, (half, rows), 1)
        g = lax.broadcasted_iota(jnp.int32, (half, rows), 0)
        same = shard_of(g) == q // 2 + k * (rows // 2)
        for side in range(2):
            block = atom if side == 0 else atom + 1 - 2 * core
            pick = (lax.broadcasted_iota(jnp.int32, (LANES, rows), 0) == block).astype(BF)
            slot = nn_dot(tags[:half], pick)
            hit = same & (slot == (q % 2).astype(F32))
            sel_t[:, side * rows : (side + 1) * rows] = jnp.where(hit, 1.0, 0.0).astype(BF)

    def chain(k):
        state = codes.at[pl.ds(k * rows, rows), :]
        sel, sel_t, start = r["sel"].at[k], r["sel_t"].at[k], r["start"].at[k]
        table, total = r["table"].at[k], r["total"].at[k]
        for it in range(ITERS):
            big = [r["g0a" if it == 0 else "g0b"].at[k], r["g1"].at[it, k]]
            part, opp, nbr = r["part"].at[it, k], r["y_opp"].at[it, k], r["y_nbr"].at[it, k]
            full, back, terms = r["full"].at[it, k], r["back"].at[it, k], r["terms"].at[it, k]
            if it == 0:
                pieces = [first[k * shards_in + j].astype(F32) for j in range(shards_in)]
                unit = jnp.concatenate(pieces, axis=0)
                start[:, :1024] = unit[:, :1024]
                start[:, 1024:] = unit[:, 1152:]
                unit = unit.astype(BF)
                big[0][0, 0, 0] = unit[:, :1152]
                big[1][0, 0, 0] = unit[:, 1152:]
            yield from gather(big)
            if it == 0:
                make_selectors(k, sel, sel_t, big)
            chosen = sel[...]
            for h in range(2):
                @pl.loop(0, 4)
                def _(n, h=h):
                    cols = pl.ds(pl.multiple_of(n * 256, 256), 256)
                    values = big[h][:, :, :, :, cols].reshape(gathered, 256)
                    out = pl.ds(pl.multiple_of(h * 1024 + n * 256, 256), 256)
                    table[:, out] = nn_dot(chosen, values).astype(BF)
            if it == 0 and k == 0:
                load.wait()

            def products(position):
                base = ((y + SHIFT[position]) % 4) * 512

                @pl.loop(0, 2)
                def _(n):
                    taken = weights[pl.ds(pl.multiple_of(base + n * 256, 256), 256), :]
                    cols = pl.ds(pl.multiple_of(n * 256, 256), 256)
                    part[position, :, cols] = nt_dot(table[...], taken).astype(BF)

            products(3)
            c_om = net.copy(part.at[3, :, lo], opp.at[0], plus["y"])
            c_op = net.copy(part.at[3, :, hi], opp.at[1], minus["y"])
            products(2)
            c_ph = net.copy(part.at[2, :, hi], nbr.at[0, :, hi], plus["y"])
            products(1)
            c_ml = net.copy(part.at[1, :, lo], nbr.at[1, :, lo], minus["y"])
            yield
            c_om.wait_recv()
            part[2, :, lo] = (part[2, :, lo].astype(F32) + opp[0].astype(F32)).astype(BF)
            c_pl = net.copy(part.at[2, :, lo], nbr.at[0, :, lo], plus["y"])
            c_op.wait_recv()
            part[1, :, hi] = (part[1, :, hi].astype(F32) + opp[1].astype(F32)).astype(BF)
            c_mh = net.copy(part.at[1, :, hi], nbr.at[1, :, hi], minus["y"])
            products(0)
            yield

            def update(cols):
                gradient = part[0, :, cols].astype(F32) + nbr[0, :, cols].astype(F32)
                gradient = gradient + nbr[1, :, cols].astype(F32)
                moved = STEP * (gradient - SPARSITY)
                if it > 0:
                    moved = moved + state[:, cols]
                moved = jnp.maximum(moved, 0.0)
                state[:, cols] = moved
                full[0, :, cols] = moved.astype(BF)

            c_ml.wait_recv()
            c_pl.wait_recv()
            update(lo)
            s1 = net.copy(full.at[0, :, lo], full.at[1, :, lo], plus["y"])
            c_ph.wait_recv()
            c_mh.wait_recv()
            update(hi)
            s2 = net.copy(full.at[0, :, hi], full.at[2, :, hi], minus["y"])
            s3 = net.copy(full.at[0, :, hi], full.at[1, :, hi], plus["y"])
            s4 = net.copy(full.at[0, :, lo], full.at[2, :, lo], minus["y"])

            def taken(position, cols):
                base = ((y + SHIFT[position]) % 4) * 512
                return weights[pl.ds(pl.multiple_of(base, 512), 512), cols]

            @pl.loop(0, 8)
            def _(n):
                cols = pl.ds(pl.multiple_of(n * 256, 256), 256)
                total[:, cols] = nn_dot(full[0], taken(0, cols))

            yield
            s1.wait_recv()
            f1 = net.copy(full.at[1, :, lo], full.at[3, :, lo], plus["y"])
            s2.wait_recv()
            f2 = net.copy(full.at[2, :, hi], full.at[3, :, hi], minus["y"])
            yield
            s3.wait_recv()
            s4.wait_recv()

            @pl.loop(0, 8)
            def _(n):
                cols = pl.ds(pl.multiple_of(n * 256, 256), 256)
                total[:, cols] += nn_dot(full[1], taken(1, cols)) + nn_dot(full[2], taken(2, cols))

            yield
            f1.wait_recv()
            f2.wait_recv()
            shared = []
            for quarter in range(4):
                @pl.loop(0, 2)
                def _(n, quarter=quarter):
                    cols = pl.ds(pl.multiple_of(quarter * 512 + n * 256, 256), 256)
                    done = total[:, cols] + nn_dot(full[3], taken(3, cols))
                    back[0, :, cols] = done.astype(BF)

                cols = pl.ds(quarter * 512, 512)
                shared.append(net.copy(back.at[0, :, cols], back.at[1, :, cols], partner))
            yield
            spread = sel_t[...]
            opp_t, nbr_t = r["t_opp"].at[it, k], r["t_nbr"].at[it, k]
            opp_u, nbr_u = r["u_opp"].at[it, k], r["u_nbr"].at[it, k]
            lines = r["lines"].at[it, k]
            sums = []
            for h in range(2):
                for made in shared[2 * h : 2 * h + 2]:
                    made.wait_recv()

                @pl.loop(0, 4)
                def _(n, h=h):
                    cols = pl.ds(pl.multiple_of(h * 1024 + n * 256, 256), 256)
                    both = nn_dot(spread[:, :rows], back[0, :, cols])
                    both = both + nn_dot(spread[:, rows:], back[1, :, cols])
                    out = pl.ds(pl.multiple_of(n * 256, 256), 256)
                    terms[h, :, :, :, out] = both.astype(BF).reshape(4, 4, tokens_in, 256)

                def term(position, cols, h=h):
                    if h == 0:
                        return terms.at[h, :, position, :, cols]
                    return terms.at[h, position, :, :, cols]

                step = ring_sum("z" if h == 0 else "x", term, opp_t.at[h], nbr_t.at[h], 1024)
                next(step)
                sums.append(step)
            yield
            for step in sums:
                next(step)
            yield
            small = []
            for h in range(2):
                for _ in sums[h]:
                    pass
                own = terms[h, :, 0] if h == 0 else terms[h, 0]
                line = own.astype(F32) + nbr_t[h, 0].astype(F32) + nbr_t[h, 1].astype(F32)
                lines[h] = line.astype(BF)

                def unit_of(position, cols, h=h):
                    return lines.at[h, position, :, cols]

                step = ring_sum("x" if h == 0 else "z", unit_of, opp_u.at[h], nbr_u.at[h], 1024)
                next(step)
                small.append(step)
            yield
            for step in small:
                next(step)
            yield
            for h in range(2):
                for _ in small[h]:
                    pass
                summed = lines[h, 0].astype(F32) + nbr_u[h, 0].astype(F32) + nbr_u[h, 1].astype(F32)
                residual = start[:, h * 1024 : (h + 1) * 1024] - summed
                if it + 1 < ITERS:
                    nxt = r["g0b"].at[k] if h == 0 else r["g1"].at[it + 1, k]
                    nxt[0, 0, 0] = residual.astype(BF)
                else:
                    for j in range(shards_in):
                        r["final"][k * shards_in + j, :, h * 1024 : (h + 1) * 1024] = residual[4 * j : 4 * j + 4]

    for made in swaps:
        made.wait_recv()
    runs = [chain(k) for k in range(CHAINS)]
    for run in runs:
        for _ in run:
            pass
    final, landed = r["final"], r["landed"]
    ends = []
    for position in (1, 2, 3):
        target = (y + SHIFT[position]) % 4
        ends.append(net.copy(final.at[target], landed.at[y], {"grp": target}))
    landed[y] = final[y]
    for made in ends:
        made.wait_recv()
    res_out[...] = landed[...]
    net.finish()


def scratch():
    t, rows, gathered = 16 // CHAINS, 256 // CHAINS, 512 // CHAINS
    c, i = CHAINS, ITERS
    v = pltpu.VMEM
    return dict(
        weights=v((2048, 2048), BF),
        first=v((4, 4, 2176), BF),
        start=v((c, t, 2048), F32),
        g0a=v((c, 2, 4, 4, t, 1152), BF),
        g0b=v((c, 2, 4, 4, t, 1024), BF),
        g1=v((i, c, 2, 4, 4, t, 1024), BF),
        sel=v((c, rows, gathered), BF),
        sel_t=v((c, gathered // 2, 2 * rows), BF),
        table=v((c, rows, 2048), BF),
        part=v((i, c, 4, rows, 512), BF),
        y_opp=v((i, c, 2, rows, 256), BF),
        y_nbr=v((i, c, 2, rows, 512), BF),
        full=v((i, c, 4, rows, 512), BF),
        total=v((c, rows, 2048), F32),
        back=v((i, c, 2, rows, 2048), BF),
        terms=v((i, c, 2, 4, 4, t, 1024), BF),
        t_opp=v((i, c, 2, 2, 4, t, 512), BF),
        t_nbr=v((i, c, 2, 2, 4, t, 1024), BF),
        lines=v((i, c, 2, 4, t, 1024), BF),
        u_opp=v((i, c, 2, 2, t, 512), BF),
        u_nbr=v((i, c, 2, 2, t, 1024), BF),
        final=v((4, 4, 2048), F32),
        landed=v((4, 4, 2048), F32),
        send=pltpu.SemaphoreType.DMA((N_SEMS,)),
        recv=pltpu.SemaphoreType.DMA((N_SEMS,)),
        wsem=pltpu.SemaphoreType.DMA,
    )


def per_device(tokens, dictionary, candidates):
    block_ids = jnp.arange(LANES, dtype=jnp.int32)
    member = jnp.any(candidates[:, :, None] == block_ids, axis=1).astype(jnp.int32)
    earlier = (jnp.arange(4)[:, None] > jnp.arange(4)[None, :]).astype(jnp.int32)
    before = jnp.sum(earlier[:, :, None] * member[None], axis=1)
    tags = jnp.where(member > 0, before, -1).astype(BF)
    parts = tokens.reshape(4, 4, 2048).swapaxes(0, 1)
    tok = jnp.concatenate(
        [parts[:, :, :1024], jnp.broadcast_to(tags, (4, 4, LANES)), parts[:, :, 1024:]], axis=2
    )
    shapes = scratch()
    names = ["tok", "dict", "res", "codes"] + list(shapes)
    vmem = pl.BlockSpec(memory_space=pltpu.VMEM)
    res, codes = pl.pallas_call(
        lambda *refs: body(names, *refs),
        out_shape=(
            jax.ShapeDtypeStruct((4, 4, 2048), F32),
            jax.ShapeDtypeStruct((256, 512), F32),
        ),
        in_specs=[vmem, pl.BlockSpec(memory_space=pl.ANY)],
        out_specs=(vmem, vmem),
        scratch_shapes=list(shapes.values()),
        compiler_params=pltpu.CompilerParams(
            collective_id=0, has_side_effects=True, vmem_limit_bytes=60 * 1024 * 1024
        ),
        name="sparse_code",
    )(tok, dictionary)
    return res.swapaxes(0, 1).reshape(4, 8192), codes[None]


def solution(mesh):
    placed = (P(("grp", "atom"), None), P("atom", None, "grp"), P(("grp", "atom"), None))
    return jax.shard_map(
        per_device,
        mesh=mesh,
        in_specs=placed,
        out_specs=(P(("grp", "atom"), None), P("atom", None, "grp")),
        check_vma=False,
    )
```

```python
import jax
import jax.numpy as jnp
from jax import lax
from jax.experimental import pallas as pl
from jax.experimental.pallas import tpu as pltpu
from jax.sharding import PartitionSpec as P

ITERS = 2
CHAINS = 1
STEP = 1.6
SPARSITY = 0.125
MESH = pl.DeviceIdType.MESH
SHIFT = (0, 3, 1, 2)
BACK = (0, 2, 1, 3)
BF = jnp.bfloat16
F32 = jnp.float32
N_SEMS = 260
LANES = 128


def nt_dot(a, b):
    return lax.dot_general(a, b, (((1,), (1,)), ((), ())), preferred_element_type=F32)


def nn_dot(a, b):
    return jnp.dot(a, b, preferred_element_type=F32)


def source(me, position):
    shift = jnp.where(position == 1, 3, jnp.where(position == 2, 1, jnp.where(position == 3, 2, 0)))
    return (me + shift) % 4


class Net:
    def __init__(self, send, recv):
        self.send, self.recv, self.count, self.open = send, recv, 0, []

    def copy(self, src, dst, device):
        n = self.count
        self.count += 1
        made = pltpu.make_async_remote_copy(
            src_ref=src,
            dst_ref=dst,
            send_sem=self.send.at[n],
            recv_sem=self.recv.at[n],
            device_id=device,
            device_id_type=MESH,
        )
        made.start()
        self.open.append(made)
        return made

    def finish(self):
        for made in self.open:
            made.wait_send()


def body(names, *refs):
    r = dict(zip(names, refs))
    tok, dict_hbm, res_out, codes = r["tok"], r["dict"], r["res"], r["codes"]
    tags = r["tags"]
    weights = r["weights"]
    y, atom = lax.axis_index("grp"), lax.axis_index("atom")
    x, z, core = atom // 8, (atom // 2) % 4, atom % 2
    tokens_in = 16 // CHAINS
    shards_in = 4 // CHAINS
    rows = 256 // CHAINS
    gathered = 32 * tokens_in
    half = gathered // 2

    load = pltpu.make_async_copy(dict_hbm.at[0], weights, r["wsem"])
    load.start()

    def device(nx, nz, nc):
        return {"atom": nx * 8 + nz * 2 + nc}

    ring = {
        "x": [device((x + d) % 4, z, core) for d in SHIFT],
        "z": [device(x, (z + d) % 4, core) for d in SHIFT],
        "y": [{"grp": (y + d) % 4} for d in SHIFT],
    }
    minus = {axis: ring[axis][1] for axis in ring}
    plus = {axis: ring[axis][2] for axis in ring}
    partner = device(x, z, 1 - core)

    barrier = pltpu.get_barrier_semaphore()
    others = ring["x"][1:] + ring["z"][1:] + ring["y"][1:] + [partner]
    for other in others:
        pl.semaphore_signal(barrier, inc=1, device_id=other, device_id_type=MESH)

    lane = lax.broadcasted_iota(jnp.int32, (4, LANES), 1)
    row = lax.broadcasted_iota(jnp.int32, (4, LANES), 0)
    named = jnp.zeros((4, LANES), jnp.int32)
    for k in range(8):
        named = named + jnp.where(r["cand"][:, k : k + 1] == lane, 1, 0)
    before = jnp.zeros((4, LANES), jnp.int32)
    for t in range(3):
        before = before + jnp.where(row > t, named[t : t + 1], 0)
    tags[...] = jnp.where(named > 0, before, -1).astype(F32).astype(BF)
    pl.semaphore_wait(barrier, len(others))

    net = Net(r["send"], r["recv"])

    first = r["first"]
    swaps = []
    for position in (1, 2, 3):
        target = (y + SHIFT[position]) % 4
        cols = pl.ds(pl.multiple_of(target * 2048, 2048), 2048)
        swaps.append(net.copy(tok.at[:, cols], first.at[y, :, pl.ds(0, 2048)], ring["y"][position]))
        swaps.append(net.copy(tags, first.at[y, :, pl.ds(2048, LANES)], ring["y"][position]))
    first[y, :, :2048] = tok[:, pl.ds(pl.multiple_of(y * 2048, 2048), 2048)]
    first[y, :, 2048:] = tags[...]

    lo, hi = pl.ds(0, 256), pl.ds(256, 256)

    def gather(big):
        st = []
        for h in range(2):
            g = big[h]
            a, b = ("x", "z") if h == 0 else ("z", "x")

            def view(pa, pb, owner=0, g=g, h=h):
                return g.at[owner, pa, pb] if h == 0 else g.at[owner, pb, pa]

            def share(pa, pb, view=view):
                return net.copy(view(pa, pb), view(pa, pb, owner=1), partner)

            st.append(dict(view=view, share=share, a=a, b=b))
        mid, rest = pl.ds(1, 2), pl.ds(1, 3)

        def spread(s, pa):
            return [net.copy(s["view"](pa, 0), s["view"](pa, d), ring[s["b"]][BACK[d]]) for d in (3, 1, 2)]

        for s in st:
            v = s["view"]
            s["near"] = [net.copy(v(0, 0), v(d, 0), ring[s["a"]][BACK[d]]) for d in (3, 1, 2)]
        for s in st:
            s["own"] = spread(s, 0)
            s["part"] = [s["share"](0, 0)]
        yield
        for s in st:
            s["near"][1].wait_recv()
            s["near"][2].wait_recv()
            s["mid"] = spread(s, mid)
        for s in st:
            s["near"][0].wait_recv()
            s["far"] = spread(s, 3)
            s["part"].append(s["share"](rest, 0))
        yield
        for s in st:
            for made in s["own"]:
                made.wait_recv()
            s["part"].append(s["share"](0, rest))
        yield
        for s in st:
            for made in s["mid"]:
                made.wait_recv()
            s["part"].append(s["share"](mid, rest))
        for s in st:
            for made in s["far"]:
                made.wait_recv()
            s["part"].append(s["share"](3, rest))
        yield
        for s in st:
            for made in s["part"]:
                made.wait_recv()

    def ring_sum(axis, view, landing):
        made = [net.copy(view(d), landing.at[BACK[d] - 1], ring[axis][d]) for d in (3, 1, 2)]
        yield
        for one in made:
            one.wait_recv()

    def shard_of(g, k):
        px, pz = (g // (4 * tokens_in)) % 4, (g // tokens_in) % 4
        own = g // (16 * tokens_in)
        column = source(x, px) * 8 + source(z, pz) * 2 + (core + own) % 2
        return ((g // 4) % shards_in + k * shards_in) * 32 + column

    def wanted_slots(k, want, want_t):
        g = lax.broadcasted_iota(jnp.int32, (8, gathered), 1)
        shard = jnp.broadcast_to(shard_of(g, k)[:1], (rows, gathered))
        p = lax.broadcasted_iota(jnp.int32, (rows, gathered), 0)
        want[...] = jnp.where(shard == (p >> 1) + k * (rows // 2), p & 1, -2).astype(F32)
        g = lax.broadcasted_iota(jnp.int32, (half, LANES), 0)
        shard = jnp.broadcast_to(shard_of(g, k)[:, :1], (half, rows))
        q = lax.broadcasted_iota(jnp.int32, (half, rows), 1)
        want_t[...] = jnp.where(shard == (q >> 1) + k * (rows // 2), q & 1, -2).astype(F32)

    def make_selectors(want, want_t, sel, sel_t, big):
        given = big[0][:, :, :, :, 1024:1152].reshape(gathered, LANES)
        pick = (lax.broadcasted_iota(jnp.int32, (rows, LANES), 1) == atom).astype(BF)
        sel[...] = jnp.where(nt_dot(pick, given) == want[...], 1.0, 0.0).astype(BF)
        for side in range(2):
            block = atom if side == 0 else atom + 1 - 2 * core
            pick = (lax.broadcasted_iota(jnp.int32, (LANES, rows), 0) == block).astype(BF)
            hit = nn_dot(given[:half], pick) == want_t[...]
            sel_t[:, side * rows : (side + 1) * rows] = jnp.where(hit, 1.0, 0.0).astype(BF)

    def chain(k):
        state = codes.at[pl.ds(k * rows, rows), :]
        sel, sel_t, start = r["sel"].at[k], r["sel_t"].at[k], r["start"].at[k]
        table, total = r["table"].at[k], r["total"].at[k]
        for it in range(ITERS):
            big = [r["g0a" if it == 0 else "g0b"].at[k], r["g1"].at[it, k]]
            part, opp, nbr = r["part"].at[it, k], r["y_opp"].at[it, k], r["y_nbr"].at[it, k]
            full, back, terms = r["full"].at[it, k], r["back"].at[it, k], r["terms"].at[it, k]
            if it == 0:
                pieces = [first[k * shards_in + j].astype(F32) for j in range(shards_in)]
                unit = jnp.concatenate(pieces, axis=0)
                start[...] = unit[:, :2048]
                unit = unit.astype(BF)
                big[0][0, 0, 0, :, :1024] = unit[:, :1024]
                big[0][0, 0, 0, :, 1024:] = unit[:, 2048:]
                big[1][0, 0, 0] = unit[:, 1024:2048]
            yield from gather(big)
            if it == 0:
                make_selectors(r["want"].at[k], r["want_t"].at[k], sel, sel_t, big)
            chosen = sel[...]
            for h in range(2):
                @pl.loop(0, 4)
                def _(n, h=h):
                    cols = pl.ds(pl.multiple_of(n * 256, 256), 256)
                    values = big[h][:, :, :, :, cols].reshape(gathered, 256)
                    out = pl.ds(pl.multiple_of(h * 1024 + n * 256, 256), 256)
                    table[:, out] = nn_dot(chosen, values).astype(BF)
            if it == 0 and k == 0:
                load.wait()

            def products(position):
                base = ((y + SHIFT[position]) % 4) * 512

                @pl.loop(0, 2)
                def _(n):
                    taken = weights[pl.ds(pl.multiple_of(base + n * 256, 256), 256), :]
                    cols = pl.ds(pl.multiple_of(n * 256, 256), 256)
                    part[position, :, cols] = nt_dot(table[...], taken).astype(BF)

            products(3)
            c_om = net.copy(part.at[3, :, lo], opp.at[0], plus["y"])
            c_op = net.copy(part.at[3, :, hi], opp.at[1], minus["y"])
            products(2)
            c_ph = net.copy(part.at[2, :, hi], nbr.at[0, :, hi], plus["y"])
            products(1)
            c_ml = net.copy(part.at[1, :, lo], nbr.at[1, :, lo], minus["y"])
            yield
            c_om.wait_recv()
            part[2, :, lo] = (part[2, :, lo].astype(F32) + opp[0].astype(F32)).astype(BF)
            c_pl = net.copy(part.at[2, :, lo], nbr.at[0, :, lo], plus["y"])
            c_op.wait_recv()
            part[1, :, hi] = (part[1, :, hi].astype(F32) + opp[1].astype(F32)).astype(BF)
            c_mh = net.copy(part.at[1, :, hi], nbr.at[1, :, hi], minus["y"])
            products(0)
            yield

            def update(cols):
                gradient = part[0, :, cols].astype(F32) + nbr[0, :, cols].astype(F32)
                gradient = gradient + nbr[1, :, cols].astype(F32)
                moved = STEP * (gradient - SPARSITY)
                if it > 0:
                    moved = moved + state[:, cols]
                moved = jnp.maximum(moved, 0.0)
                state[:, cols] = moved
                full[0, :, cols] = moved.astype(BF)

            c_ml.wait_recv()
            c_pl.wait_recv()
            update(lo)
            s1 = net.copy(full.at[0, :, lo], full.at[1, :, lo], plus["y"])
            c_ph.wait_recv()
            c_mh.wait_recv()
            update(hi)
            s2 = net.copy(full.at[0, :, hi], full.at[2, :, hi], minus["y"])
            s3 = net.copy(full.at[0, :, hi], full.at[1, :, hi], plus["y"])
            s4 = net.copy(full.at[0, :, lo], full.at[2, :, lo], minus["y"])

            def taken(position, cols):
                base = ((y + SHIFT[position]) % 4) * 512
                return weights[pl.ds(pl.multiple_of(base, 512), 512), cols]

            @pl.loop(0, 8)
            def _(n):
                cols = pl.ds(pl.multiple_of(n * 256, 256), 256)
                total[:, cols] = nn_dot(full[0], taken(0, cols))

            yield
            s1.wait_recv()
            f1 = net.copy(full.at[1, :, lo], full.at[3, :, lo], plus["y"])
            s2.wait_recv()
            f2 = net.copy(full.at[2, :, hi], full.at[3, :, hi], minus["y"])
            yield
            s3.wait_recv()
            s4.wait_recv()

            @pl.loop(0, 8)
            def _(n):
                cols = pl.ds(pl.multiple_of(n * 256, 256), 256)
                total[:, cols] += nn_dot(full[1], taken(1, cols)) + nn_dot(full[2], taken(2, cols))

            yield
            f1.wait_recv()
            f2.wait_recv()
            shared = []
            for quarter in range(4):
                @pl.loop(0, 2)
                def _(n, quarter=quarter):
                    cols = pl.ds(pl.multiple_of(quarter * 512 + n * 256, 256), 256)
                    done = total[:, cols] + nn_dot(full[3], taken(3, cols))
                    back[0, :, cols] = done.astype(BF)

                cols = pl.ds(quarter * 512, 512)
                shared.append(net.copy(back.at[0, :, cols], back.at[1, :, cols], partner))
            yield
            spread = sel_t[...]
            nbr_t, nbr_u, lines = r["t_nbr"].at[it, k], r["u_nbr"].at[it, k], r["lines"].at[it, k]
            sums = []
            for h in range(2):
                for made in shared[2 * h : 2 * h + 2]:
                    made.wait_recv()

                @pl.loop(0, 4)
                def _(n, h=h):
                    cols = pl.ds(pl.multiple_of(h * 1024 + n * 256, 256), 256)
                    both = nn_dot(spread[:, :rows], back[0, :, cols])
                    both = both + nn_dot(spread[:, rows:], back[1, :, cols])
                    out = pl.ds(pl.multiple_of(n * 256, 256), 256)
                    terms[h, :, :, :, out] = both.astype(BF).reshape(4, 4, tokens_in, 256)

                def term(position, h=h):
                    return terms.at[h, :, position] if h == 0 else terms.at[h, position]

                step = ring_sum("z" if h == 0 else "x", term, nbr_t.at[h])
                next(step)
                sums.append(step)
            yield
            small = []
            for h in range(2):
                for _ in sums[h]:
                    pass
                line = (terms[h, :, 0] if h == 0 else terms[h, 0]).astype(F32)
                for d in range(3):
                    line = line + nbr_t[h, d].astype(F32)
                lines[h] = line.astype(BF)

                def unit_of(position, h=h):
                    return lines.at[h, position]

                step = ring_sum("x" if h == 0 else "z", unit_of, nbr_u.at[h])
                next(step)
                small.append(step)
            yield
            for h in range(2):
                for _ in small[h]:
                    pass
                summed = lines[h, 0].astype(F32)
                for d in range(3):
                    summed = summed + nbr_u[h, d].astype(F32)
                residual = start[:, h * 1024 : (h + 1) * 1024] - summed
                if it + 1 < ITERS:
                    nxt = r["g0b"].at[k] if h == 0 else r["g1"].at[it + 1, k]
                    nxt[0, 0, 0] = residual.astype(BF)
                else:
                    for j in range(shards_in):
                        r["final"][k * shards_in + j, :, h * 1024 : (h + 1) * 1024] = residual[4 * j : 4 * j + 4]

    for k in range(CHAINS):
        wanted_slots(k, r["want"].at[k], r["want_t"].at[k])
    for made in swaps:
        made.wait_recv()
    runs = [chain(k) for k in range(CHAINS)]
    for run in runs:
        for _ in run:
            pass
    final, landed = r["final"], r["landed"]
    ends = []
    for position in (1, 2, 3):
        target = (y + SHIFT[position]) % 4
        ends.append(net.copy(final.at[target], landed.at[y], ring["y"][position]))
    landed[y] = final[y]
    for made in ends:
        made.wait_recv()
    for q in range(4):
        res_out[:, q * 2048 : (q + 1) * 2048] = landed[q]
    net.finish()


def scratch():
    t, rows, gathered = 16 // CHAINS, 256 // CHAINS, 512 // CHAINS
    c, i = CHAINS, ITERS
    v = pltpu.VMEM
    return dict(
        weights=v((2048, 2048), BF),
        first=v((4, 4, 2176), BF),
        start=v((c, t, 2048), F32),
        g0a=v((c, 2, 4, 4, t, 1152), BF),
        g0b=v((c, 2, 4, 4, t, 1024), BF),
        g1=v((i, c, 2, 4, 4, t, 1024), BF),
        sel=v((c, rows, gathered), BF),
        sel_t=v((c, gathered // 2, 2 * rows), BF),
        table=v((c, rows, 2048), BF),
        part=v((i, c, 4, rows, 512), BF),
        y_opp=v((i, c, 2, rows, 256), BF),
        y_nbr=v((i, c, 2, rows, 512), BF),
        full=v((i, c, 4, rows, 512), BF),
        total=v((c, rows, 2048), F32),
        back=v((i, c, 2, rows, 2048), BF),
        terms=v((i, c, 2, 4, 4, t, 1024), BF),
        t_nbr=v((i, c, 2, 3, 4, t, 1024), BF),
        lines=v((i, c, 2, 4, t, 1024), BF),
        u_nbr=v((i, c, 2, 3, t, 1024), BF),
        tags=v((4, LANES), BF),
        want=v((c, rows, gathered), F32),
        want_t=v((c, gathered // 2, rows), F32),
        final=v((4, 4, 2048), F32),
        landed=v((4, 4, 2048), F32),
        send=pltpu.SemaphoreType.DMA((N_SEMS,)),
        recv=pltpu.SemaphoreType.DMA((N_SEMS,)),
        wsem=pltpu.SemaphoreType.DMA,
    )


def per_device(tokens, dictionary, candidates):
    shapes = scratch()
    names = ["tok", "dict", "cand", "res", "codes"] + list(shapes)
    vmem = pl.BlockSpec(memory_space=pltpu.VMEM)
    res, codes = pl.pallas_call(
        lambda *refs: body(names, *refs),
        out_shape=(
            jax.ShapeDtypeStruct((4, 8192), F32),
            jax.ShapeDtypeStruct((256, 512), F32),
        ),
        in_specs=[vmem, pl.BlockSpec(memory_space=pl.ANY), vmem],
        out_specs=(vmem, vmem),
        scratch_shapes=list(shapes.values()),
        compiler_params=pltpu.CompilerParams(
            collective_id=0, has_side_effects=True, vmem_limit_bytes=60 * 1024 * 1024
        ),
        name="sparse_code",
    )(tokens, dictionary, candidates)
    return res, codes[None]


def solution(mesh):
    placed = (P(("grp", "atom"), None), P("atom", None, "grp"), P(("grp", "atom"), None))
    return jax.shard_map(
        per_device,
        mesh=mesh,
        in_specs=placed,
        out_specs=(P(("grp", "atom"), None), P("atom", None, "grp")),
        check_vma=False,
    )
```

```python
import jax
import jax.numpy as jnp
from jax import lax
from jax.experimental import pallas as pl
from jax.experimental.pallas import tpu as pltpu
from jax.sharding import PartitionSpec as P

ITERS = 2
CHAINS = 1
STEP = 1.6
SPARSITY = 0.125
MESH = pl.DeviceIdType.MESH
SHIFT = (0, 3, 1, 2)
BACK = (0, 2, 1, 3)
BF = jnp.bfloat16
F32 = jnp.float32
N_SEMS = 260
LANES = 128


def nt_dot(a, b):
    return lax.dot_general(a, b, (((1,), (1,)), ((), ())), preferred_element_type=F32)


def nn_dot(a, b):
    return jnp.dot(a, b, preferred_element_type=F32)


def source(me, position):
    shift = jnp.where(position == 1, 3, jnp.where(position == 2, 1, jnp.where(position == 3, 2, 0)))
    return (me + shift) % 4


class Net:
    def __init__(self, send, recv):
        self.send, self.recv, self.count, self.open = send, recv, 0, []

    def copy(self, src, dst, device):
        n = self.count
        self.count += 1
        made = pltpu.make_async_remote_copy(
            src_ref=src,
            dst_ref=dst,
            send_sem=self.send.at[n],
            recv_sem=self.recv.at[n],
            device_id=device,
            device_id_type=MESH,
        )
        made.start()
        self.open.append(made)
        return made

    def finish(self):
        for made in self.open:
            made.wait_send()


def body(names, *refs):
    r = dict(zip(names, refs))
    tok, dict_hbm, res_out, codes = r["tok"], r["dict"], r["res"], r["codes"]
    tags = r["tags"]
    weights = r["weights"]
    y, atom = lax.axis_index("grp"), lax.axis_index("atom")
    x, z, core = atom // 8, (atom // 2) % 4, atom % 2
    tokens_in = 16 // CHAINS
    shards_in = 4 // CHAINS
    rows = 256 // CHAINS
    gathered = 32 * tokens_in
    half = gathered // 2

    load = pltpu.make_async_copy(dict_hbm.at[0], weights, r["wsem"])
    load.start()

    def device(nx, nz, nc):
        return {"atom": nx * 8 + nz * 2 + nc}

    ring = {
        "x": [device((x + d) % 4, z, core) for d in SHIFT],
        "z": [device(x, (z + d) % 4, core) for d in SHIFT],
        "y": [{"grp": (y + d) % 4} for d in SHIFT],
    }
    minus = {axis: ring[axis][1] for axis in ring}
    plus = {axis: ring[axis][2] for axis in ring}
    partner = device(x, z, 1 - core)

    barrier = pltpu.get_barrier_semaphore()
    others = ring["x"][1:] + ring["z"][1:] + ring["y"][1:] + [partner]
    for other in others:
        pl.semaphore_signal(barrier, inc=1, device_id=other, device_id_type=MESH)

    lane = lax.broadcasted_iota(jnp.int32, (4, LANES), 1)
    row = lax.broadcasted_iota(jnp.int32, (4, LANES), 0)
    named = jnp.zeros((4, LANES), jnp.int32)
    for k in range(8):
        named = named + jnp.where(r["cand"][:, k : k + 1] == lane, 1, 0)
    before = jnp.zeros((4, LANES), jnp.int32)
    for t in range(3):
        before = before + jnp.where(row > t, named[t : t + 1], 0)
    tags[...] = jnp.where(named > 0, before, -1).astype(F32).astype(BF)
    pl.semaphore_wait(barrier, len(others))

    net = Net(r["send"], r["recv"])

    first = r["first"]
    swaps = []
    for position in (1, 2, 3):
        target = (y + SHIFT[position]) % 4
        cols = pl.ds(pl.multiple_of(target * 2048, 2048), 2048)
        swaps.append(net.copy(tok.at[:, cols], first.at[y, :, pl.ds(0, 2048)], ring["y"][position]))
        swaps.append(net.copy(tags, first.at[y, :, pl.ds(2048, LANES)], ring["y"][position]))
    first[y, :, :2048] = tok[:, pl.ds(pl.multiple_of(y * 2048, 2048), 2048)]
    first[y, :, 2048:] = tags[...]

    lo, hi = pl.ds(0, 256), pl.ds(256, 256)

    def gather(big):
        st = []
        for h in range(2):
            g = big[h]
            a, b = ("x", "z") if h == 0 else ("z", "x")

            def view(pa, pb, owner=0, g=g, h=h):
                return g.at[owner, pa, pb] if h == 0 else g.at[owner, pb, pa]

            def share(pa, pb, view=view):
                return net.copy(view(pa, pb), view(pa, pb, owner=1), partner)

            st.append(dict(view=view, share=share, a=a, b=b))
        mid, rest = pl.ds(1, 2), pl.ds(1, 3)

        def spread(s, pa):
            return [net.copy(s["view"](pa, 0), s["view"](pa, d), ring[s["b"]][BACK[d]]) for d in (3, 1, 2)]

        for s in st:
            v = s["view"]
            s["near"] = [net.copy(v(0, 0), v(d, 0), ring[s["a"]][BACK[d]]) for d in (3, 1, 2)]
        for s in st:
            s["own"] = spread(s, 0)
            s["part"] = [s["share"](0, 0)]
        yield
        for s in st:
            s["near"][1].wait_recv()
            s["near"][2].wait_recv()
            s["mid"] = spread(s, mid)
        for s in st:
            s["near"][0].wait_recv()
            s["far"] = spread(s, 3)
            s["part"].append(s["share"](rest, 0))
        yield
        for s in st:
            for made in s["own"]:
                made.wait_recv()
            s["part"].append(s["share"](0, rest))
        yield
        for group, pa in (("mid", mid), ("far", 3)):
            for i, d in ((1, 1), (2, 2), (0, 3)):
                for s in st:
                    s[group][i].wait_recv()
                    s["part"].append(s["share"](pa, d))
        yield
        for s in st:
            for made in s["part"]:
                made.wait_recv()

    def ring_sum(axis, view, landing):
        return [net.copy(view(d), landing(BACK[d] - 1), ring[axis][d]) for d in (3, 1, 2)]

    def shard_of(g, k):
        px, pz = (g // (4 * tokens_in)) % 4, (g // tokens_in) % 4
        own = g // (16 * tokens_in)
        column = source(x, px) * 8 + source(z, pz) * 2 + (core + own) % 2
        return ((g // 4) % shards_in + k * shards_in) * 32 + column

    def wanted_slots(k, want, want_t):
        g = lax.broadcasted_iota(jnp.int32, (8, gathered), 1)
        shard = jnp.broadcast_to(shard_of(g, k)[:1], (rows, gathered))
        p = lax.broadcasted_iota(jnp.int32, (rows, gathered), 0)
        want[...] = jnp.where(shard == (p >> 1) + k * (rows // 2), p & 1, -2).astype(F32)
        g = lax.broadcasted_iota(jnp.int32, (half, LANES), 0)
        shard = jnp.broadcast_to(shard_of(g, k)[:, :1], (half, rows))
        q = lax.broadcasted_iota(jnp.int32, (half, rows), 1)
        want_t[...] = jnp.where(shard == (q >> 1) + k * (rows // 2), q & 1, -2).astype(F32)

    def make_selectors(want, want_t, sel, sel_t, big):
        given = big[0][:, :, :, :, 1024:1152].reshape(gathered, LANES)
        pick = (lax.broadcasted_iota(jnp.int32, (rows, LANES), 1) == atom).astype(BF)
        sel[...] = jnp.where(nt_dot(pick, given) == want[...], 1.0, 0.0).astype(BF)
        for side in range(2):
            block = atom if side == 0 else atom + 1 - 2 * core
            pick = (lax.broadcasted_iota(jnp.int32, (LANES, rows), 0) == block).astype(BF)
            hit = nn_dot(given[:half], pick) == want_t[...]
            sel_t[:, side * rows : (side + 1) * rows] = jnp.where(hit, 1.0, 0.0).astype(BF)

    def chain(k):
        state = codes.at[pl.ds(k * rows, rows), :]
        sel, sel_t, start = r["sel"].at[k], r["sel_t"].at[k], r["start"].at[k]
        table, total = r["table"].at[k], r["total"].at[k]
        for it in range(ITERS):
            big = [r["g0a" if it == 0 else "g0b"].at[k], r["g1"].at[it, k]]
            part, opp, nbr = r["part"].at[it, k], r["y_opp"].at[it, k], r["y_nbr"].at[it, k]
            full, back, terms = r["full"].at[it, k], r["back"].at[it, k], r["terms"].at[it, k]
            if it == 0:
                pieces = [first[k * shards_in + j].astype(F32) for j in range(shards_in)]
                unit = jnp.concatenate(pieces, axis=0)
                start[...] = unit[:, :2048]
                unit = unit.astype(BF)
                big[0][0, 0, 0, :, :1024] = unit[:, :1024]
                big[0][0, 0, 0, :, 1024:] = unit[:, 2048:]
                big[1][0, 0, 0] = unit[:, 1024:2048]
            yield from gather(big)
            if it == 0:
                make_selectors(r["want"].at[k], r["want_t"].at[k], sel, sel_t, big)
            chosen = sel[...]
            for h in range(2):
                @pl.loop(0, 4, unroll=True)
                def _(n, h=h):
                    cols = pl.ds(pl.multiple_of(n * 256, 256), 256)
                    values = big[h][:, :, :, :, cols].reshape(gathered, 256)
                    out = pl.ds(pl.multiple_of(h * 1024 + n * 256, 256), 256)
                    table[:, out] = nn_dot(chosen, values).astype(BF)
            if it == 0 and k == 0:
                load.wait()

            def products(position):
                base = ((y + SHIFT[position]) % 4) * 512

                @pl.loop(0, 2, unroll=True)
                def _(n):
                    taken = weights[pl.ds(pl.multiple_of(base + n * 256, 256), 256), :]
                    cols = pl.ds(pl.multiple_of(n * 256, 256), 256)
                    part[position, :, cols] = nt_dot(table[...], taken).astype(BF)

            products(3)
            c_om = net.copy(part.at[3, :, lo], opp.at[0], plus["y"])
            c_op = net.copy(part.at[3, :, hi], opp.at[1], minus["y"])
            products(2)
            c_ph = net.copy(part.at[2, :, hi], nbr.at[0, :, hi], plus["y"])
            products(1)
            c_ml = net.copy(part.at[1, :, lo], nbr.at[1, :, lo], minus["y"])
            yield
            c_om.wait_recv()
            part[2, :, lo] = (part[2, :, lo].astype(F32) + opp[0].astype(F32)).astype(BF)
            c_pl = net.copy(part.at[2, :, lo], nbr.at[0, :, lo], plus["y"])
            c_op.wait_recv()
            part[1, :, hi] = (part[1, :, hi].astype(F32) + opp[1].astype(F32)).astype(BF)
            c_mh = net.copy(part.at[1, :, hi], nbr.at[1, :, hi], minus["y"])
            products(0)
            yield

            def update(cols):
                gradient = part[0, :, cols].astype(F32) + nbr[0, :, cols].astype(F32)
                gradient = gradient + nbr[1, :, cols].astype(F32)
                moved = STEP * (gradient - SPARSITY)
                if it > 0:
                    moved = moved + state[:, cols]
                if it + 1 == ITERS:
                    state[:, cols] = moved
                moved = jnp.maximum(moved, 0.0)
                if it + 1 < ITERS:
                    state[:, cols] = moved
                full[0, :, cols] = moved.astype(BF)

            c_ml.wait_recv()
            c_pl.wait_recv()
            update(lo)
            s1 = net.copy(full.at[0, :, lo], full.at[1, :, lo], plus["y"])
            c_ph.wait_recv()
            c_mh.wait_recv()
            update(hi)
            s2 = net.copy(full.at[0, :, hi], full.at[2, :, hi], minus["y"])
            s3 = net.copy(full.at[0, :, hi], full.at[1, :, hi], plus["y"])
            s4 = net.copy(full.at[0, :, lo], full.at[2, :, lo], minus["y"])

            def taken(position, cols):
                base = ((y + SHIFT[position]) % 4) * 512
                return weights[pl.ds(pl.multiple_of(base, 512), 512), cols]

            @pl.loop(0, 8, unroll=True)
            def _(n):
                cols = pl.ds(pl.multiple_of(n * 256, 256), 256)
                total[:, cols] = nn_dot(full[0], taken(0, cols))

            yield
            s1.wait_recv()
            f1 = net.copy(full.at[1, :, lo], full.at[3, :, lo], plus["y"])
            s2.wait_recv()
            f2 = net.copy(full.at[2, :, hi], full.at[3, :, hi], minus["y"])
            yield
            s3.wait_recv()
            s4.wait_recv()

            @pl.loop(0, 8, unroll=True)
            def _(n):
                cols = pl.ds(pl.multiple_of(n * 256, 256), 256)
                total[:, cols] += nn_dot(full[1], taken(1, cols)) + nn_dot(full[2], taken(2, cols))

            yield
            f1.wait_recv()
            f2.wait_recv()
            shared = []
            for quarter in range(4):
                @pl.loop(0, 2, unroll=True)
                def _(n, quarter=quarter):
                    cols = pl.ds(pl.multiple_of(quarter * 512 + n * 256, 256), 256)
                    done = total[:, cols] + nn_dot(full[3], taken(3, cols))
                    back[0, :, cols] = done.astype(BF)

                cols = pl.ds(quarter * 512, 512)
                shared.append(net.copy(back.at[0, :, cols], back.at[1, :, cols], partner))
            yield
            spread = sel_t[...]
            nbr_t, nbr_u, lines = r["t_nbr"].at[it, k], r["u_nbr"].at[it, k], r["lines"].at[it, k]
            sums = []
            for h in range(2):
                for made in shared[2 * h : 2 * h + 2]:
                    made.wait_recv()

                @pl.loop(0, 4, unroll=True)
                def _(n, h=h):
                    cols = pl.ds(pl.multiple_of(h * 1024 + n * 256, 256), 256)
                    both = nn_dot(spread[:, :rows], back[0, :, cols])
                    both = both + nn_dot(spread[:, rows:], back[1, :, cols])
                    out = pl.ds(pl.multiple_of(n * 256, 256), 256)
                    terms[h, :, :, :, out] = both.astype(BF).reshape(4, 4, tokens_in, 256)

                rest = pl.ds(1, 3)
                turn = []
                for lead in (rest, 0):

                    def term(position, h=h, lead=lead):
                        return terms.at[h, lead, position] if h == 0 else terms.at[h, position, lead]

                    def land(side, h=h, lead=lead):
                        return nbr_t.at[h, side, lead]

                    turn.append(ring_sum("z" if h == 0 else "x", term, land))
                sums.append(turn)
            yield
            small = []
            for h in range(2):
                for made in sums[h][0]:
                    made.wait_recv()
                line = (terms[h, 1:4, 0] if h == 0 else terms[h, 0, 1:4]).astype(F32)
                for d in range(3):
                    line = line + nbr_t[h, d, 1:4].astype(F32)
                lines[h, 1:4] = line.astype(BF)

                def unit_of(position, h=h):
                    return lines.at[h, position]

                def land(side, h=h):
                    return nbr_u.at[h, side]

                small.append(ring_sum("x" if h == 0 else "z", unit_of, land))
            yield
            for h in range(2):
                for made in sums[h][1]:
                    made.wait_recv()
                summed = terms[h, 0, 0].astype(F32)
                for d in range(3):
                    summed = summed + nbr_t[h, d, 0].astype(F32)
                for made in small[h]:
                    made.wait_recv()
                for d in range(3):
                    summed = summed + nbr_u[h, d].astype(F32)
                if it + 1 < ITERS:
                    residual = start[:, h * 1024 : (h + 1) * 1024] - summed
                    nxt = r["g0b"].at[k] if h == 0 else r["g1"].at[it + 1, k]
                    nxt[0, 0, 0] = residual.astype(BF)
                else:
                    for j in range(shards_in):
                        r["final"][k * shards_in + j, :, h * 1024 : (h + 1) * 1024] = summed[4 * j : 4 * j + 4]

    for k in range(CHAINS):
        wanted_slots(k, r["want"].at[k], r["want_t"].at[k])
    for made in swaps:
        made.wait_recv()
    runs = [chain(k) for k in range(CHAINS)]
    for run in runs:
        for _ in run:
            pass
    final, landed = r["final"], r["landed"]
    ends = []
    for position in (1, 2, 3):
        target = (y + SHIFT[position]) % 4
        ends.append(net.copy(final.at[target], landed.at[y], ring["y"][position]))
    landed[y] = final[y]
    for made in ends:
        made.wait_recv()
    for q in range(4):
        res_out[:, q * 2048 : (q + 1) * 2048] = landed[q]
    net.finish()


def scratch():
    t, rows, gathered = 16 // CHAINS, 256 // CHAINS, 512 // CHAINS
    c, i = CHAINS, ITERS
    v = pltpu.VMEM
    return dict(
        weights=v((2048, 2048), BF),
        first=v((4, 4, 2176), BF),
        start=v((c, t, 2048), F32),
        g0a=v((c, 2, 4, 4, t, 1152), BF),
        g0b=v((c, 2, 4, 4, t, 1024), BF),
        g1=v((i, c, 2, 4, 4, t, 1024), BF),
        sel=v((c, rows, gathered), BF),
        sel_t=v((c, gathered // 2, 2 * rows), BF),
        table=v((c, rows, 2048), BF),
        part=v((i, c, 4, rows, 512), BF),
        y_opp=v((i, c, 2, rows, 256), BF),
        y_nbr=v((i, c, 2, rows, 512), BF),
        full=v((i, c, 4, rows, 512), BF),
        total=v((c, rows, 2048), F32),
        back=v((i, c, 2, rows, 2048), BF),
        terms=v((i, c, 2, 4, 4, t, 1024), BF),
        t_nbr=v((i, c, 2, 3, 4, t, 1024), BF),
        lines=v((i, c, 2, 4, t, 1024), BF),
        u_nbr=v((i, c, 2, 3, t, 1024), BF),
        tags=v((4, LANES), BF),
        want=v((c, rows, gathered), F32),
        want_t=v((c, gathered // 2, rows), F32),
        final=v((4, 4, 2048), F32),
        landed=v((4, 4, 2048), F32),
        send=pltpu.SemaphoreType.DMA((N_SEMS,)),
        recv=pltpu.SemaphoreType.DMA((N_SEMS,)),
        wsem=pltpu.SemaphoreType.DMA,
    )


def per_device(tokens, dictionary, candidates):
    shapes = scratch()
    names = ["tok", "dict", "cand", "res", "codes"] + list(shapes)
    vmem = pl.BlockSpec(memory_space=pltpu.VMEM)
    rebuilt, codes = pl.pallas_call(
        lambda *refs: body(names, *refs),
        out_shape=(
            jax.ShapeDtypeStruct((4, 8192), F32),
            jax.ShapeDtypeStruct((256, 512), F32),
        ),
        in_specs=[vmem, pl.BlockSpec(memory_space=pl.ANY), vmem],
        out_specs=(vmem, vmem),
        scratch_shapes=list(shapes.values()),
        compiler_params=pltpu.CompilerParams(
            collective_id=0, has_side_effects=True, vmem_limit_bytes=60 * 1024 * 1024
        ),
        name="sparse_code",
    )(tokens, dictionary, candidates)
    return tokens.astype(F32) - rebuilt, jnp.maximum(codes, 0.0)[None]


def solution(mesh):
    placed = (P(("grp", "atom"), None), P("atom", None, "grp"), P(("grp", "atom"), None))
    return jax.shard_map(
        per_device,
        mesh=mesh,
        in_specs=placed,
        out_specs=(P(("grp", "atom"), None), P("atom", None, "grp")),
        check_vma=False,
    )
```
